32 devices in a mesh: section: 4 (over z), tensor: 8 (over y, x, core).
Axes of the slice: x: 2, y: 2, z: 4, core: 2. Of those that a mesh axis runs over, the one named last changes fastest.
Arguments:
- hidden: bfloat16 [32, 8192], P('section', 'tensor'), may hold values from -33 to 33, as said below
- out_weight: bfloat16 [4096, 8192], P(('section', 'tensor')), may hold values from -12 to 12, as said below
- targets: int32 [32], replicated, may hold values from 0 to 4095
- token_mask: int32 [32], replicated, may hold values 0 or 1
Outputs:
- ce_loss: float32 [], replicated
- z_loss: float32 [], replicated
- grad_hidden: float32 [32, 8192], P('section', 'tensor')
- grad_weight: bfloat16 [4096, 8192], P(('section', 'tensor'))
The draws below stay inside these ranges and needn't reach their ends.
Inputs may be any that keep to these rules, and one draw needn't show every extreme that they name: hidden rows of one token have one scale; entries are bounded. `out_weight`: entries are bounded.
All inputs are finite; a program needn't handle non-finite values.
Results may differ from the reference program's by a relative error of at most 0.0026.
Values may be sent and summed in bfloat16 or wider, within the bound.
No kernel may reach another device: no remote copies, remote signals or barrier semaphores. Data moves between devices by JAX's collectives and lax.ppermute only.
A program may use at most 64 MiB of HBM per device.

```python
import math
import jax
import jax.numpy as jnp
from jax import lax

D = 8192
V_DEV = 128
TOKENS = 32
VOCAB = 4096


def draw_hidden(key, part):
    scale_key, value_key = jax.random.split(jax.random.fold_in(key, 11))
    row_scale = jnp.exp(jax.random.uniform(scale_key, (TOKENS, 1), jnp.float32, 0.0, math.log(10.0))) * 0.8
    values_base = jax.random.truncated_normal(value_key, -4.0, 4.0, (TOKENS, D), jnp.float32)
    result = values_base * row_scale
    return result.astype(jnp.bfloat16)


def draw_out_weight(key, part):
    scale_key, value_key = jax.random.split(jax.random.fold_in(key, 13))
    vocab_ids = jnp.arange(VOCAB)
    vocab_ramp = 1.0 + 2.0 * vocab_ids.astype(jnp.float32) / VOCAB
    row_scale = jnp.exp(jax.random.uniform(scale_key, (VOCAB, 1), jnp.float32, math.log(0.2), math.log(2.0)))
    row_scale = row_scale * vocab_ramp[:, None] / math.sqrt(D)
    values_base = jax.random.truncated_normal(value_key, -4.0, 4.0, (VOCAB, D), jnp.float32)
    result = values_base * row_scale
    return result.astype(jnp.bfloat16)


def plant(values, own_key, low, top_value):
    longest = values.shape.index(max(values.shape))
    spots = []
    for shift in (0, 1):
        where = [jax.random.randint(jax.random.fold_in(own_key, axis), (), 0, length) for axis, length in enumerate(values.shape)]
        where[longest] = (where[longest] + shift) % values.shape[longest]
        spots.append(tuple(where))
    return values.at[spots[0]].set(low).at[spots[1]].set(top_value)


def setup_inputs(seed: int = 0) -> dict:
    key_of = jax.random.split(jax.random.key(seed), 5)
    hidden = draw_hidden(jax.random.fold_in(key_of[4], 71), 0)
    out_weight = draw_out_weight(jax.random.fold_in(key_of[4], 71), 0)
    targets = plant(jax.random.randint(key_of[2], (TOKENS,), 0, VOCAB), jax.random.fold_in(key_of[2], 1), 0, VOCAB - 1).astype(jnp.int32)
    token_mask = plant((jax.random.randint(key_of[3], (TOKENS,), 0, 4) < 3).astype(jnp.int32), jax.random.fold_in(key_of[3], 1), 0, 1)
    return dict(hidden=hidden, out_weight=out_weight, targets=targets, token_mask=token_mask)


z_weight = 1e-4


def reference(hidden, out_weight, targets, token_mask):
    logits = lax.dot_general(hidden, out_weight, (((1,), (1,)), ((), ())), preferred_element_type=jnp.float32)
    row_top = jnp.max(logits, axis=1)
    row_total = jnp.sum(jnp.exp(logits - row_top[:, None]), axis=1)
    log_total = row_top + jnp.log(row_total)
    vocab_ids = jnp.arange(VOCAB, dtype=jnp.int32)
    target_hit = targets.astype(jnp.int32)[:, None] == vocab_ids[None, :]
    picked = jnp.sum(jnp.where(target_hit, logits, 0.0), axis=1)
    kept = token_mask.astype(jnp.float32)
    ce_loss = jnp.sum(kept * (log_total - picked)) / TOKENS
    z_loss = jnp.sum(kept * log_total * log_total) / TOKENS
    factor = 1.0 + 2.0 * z_weight * log_total
    probs = jnp.exp(logits - log_total[:, None])
    dlogits = (kept[:, None] * (factor[:, None] * probs - target_hit.astype(jnp.float32))).astype(jnp.bfloat16)
    grad_hidden = jnp.dot(dlogits, out_weight, preferred_element_type=jnp.float32)
    blocks = dlogits.T.reshape(VOCAB // V_DEV, V_DEV, TOKENS)

    def weight_block(piece):
        return jnp.dot(piece, hidden, preferred_element_type=jnp.float32).astype(jnp.bfloat16)

    grad_weight = lax.map(weight_block, blocks).reshape(VOCAB, D)
    return ce_loss, z_loss, grad_hidden, grad_weight
```

```python
import jax
import jax.numpy as jnp
from jax import lax
from jax.sharding import PartitionSpec as P

z_weight = 0.0001
BOTH = ("section", "tensor")


def body(hidden, out_weight, targets, token_mask):
    sections, tensors = lax.axis_size("section"), lax.axis_size("tensor")
    devices = sections * tensors
    vocab_dev = out_weight.shape[0]
    rows, block = hidden.shape
    half = block // 2
    token_count = sections * rows
    core = lax.axis_index("tensor") % 2
    swap = [(i, i ^ 1) for i in range(tensors)]

    halves = hidden.reshape(rows, 2, half).transpose(1, 0, 2)
    sent = jnp.broadcast_to(halves[None], (devices // 2, 2, rows, half)).reshape(devices, rows, half)
    mine = lax.all_to_all(sent, BOTH, 0, 0)
    other = lax.ppermute(mine, "tensor", swap)
    low = jnp.where(core == 0, mine, other)
    high = jnp.where(core == 0, other, mine)
    gathered = jnp.stack([low, high], axis=2).reshape(sections, tensors, rows, 2, half)
    gathered = gathered.transpose(0, 2, 1, 3, 4).reshape(token_count, tensors * block)

    logits = lax.dot_general(
        gathered, out_weight, (((1,), (1,)), ((), ())), preferred_element_type=jnp.float32
    )
    vocab_start = (lax.axis_index("section") * tensors + lax.axis_index("tensor")) * vocab_dev
    local_ids = targets - vocab_start
    target_hit = local_ids[:, None] == jnp.arange(vocab_dev, dtype=jnp.int32)[None, :]
    picked_local = jnp.sum(jnp.where(target_hit, logits, 0.0), axis=1)
    local_top = jnp.max(logits, axis=1)
    local_total = jnp.sum(jnp.exp(logits - local_top[:, None]), axis=1)

    stats = jnp.concatenate([local_top, local_total, picked_local])
    width = -(-stats.shape[0] // 128) * 128
    stats = jnp.pad(stats, (0, width - stats.shape[0]))
    stats = jnp.broadcast_to(stats, (devices, 1, width))
    stats = lax.all_to_all(stats, BOTH, 0, 0).reshape(devices, width)
    tops = stats[:, :token_count]
    totals = stats[:, token_count : 2 * token_count]
    picked = jnp.sum(stats[:, 2 * token_count : 3 * token_count], axis=0)
    row_top = jnp.max(tops, axis=0)
    row_total = jnp.sum(totals * jnp.exp(tops - row_top[None, :]), axis=0)
    log_total = row_top + jnp.log(row_total)

    kept = token_mask.astype(jnp.float32)
    ce_loss = jnp.sum(kept * (log_total - picked)) / token_count
    z_loss = jnp.sum(kept * log_total * log_total) / token_count
    factor = 1.0 + 2.0 * z_weight * log_total
    probs = jnp.exp(logits - log_total[:, None])
    dlogits = (kept[:, None] * (factor[:, None] * probs - target_hit.astype(jnp.float32))).astype(
        jnp.bfloat16
    )
    grad_weight = lax.dot_general(
        dlogits, gathered, (((0,), (0,)), ((), ())), preferred_element_type=jnp.float32
    ).astype(jnp.bfloat16)

    partial = lax.dot_general(
        dlogits, out_weight, (((1,), (0,)), ((), ())), preferred_element_type=jnp.float32
    ).reshape(sections, rows, tensors, 2, half)
    first, second = partial[:, :, :, 0], partial[:, :, :, 1]
    given = jnp.where(core == 0, second, first)
    pair = jnp.where(core == 0, first, second) + lax.ppermute(given, "tensor", swap)
    pair = pair.astype(jnp.bfloat16).transpose(0, 2, 1, 3).reshape(devices, rows, half)
    shares = lax.all_to_all(pair, BOTH, 0, 0).reshape(devices // 2, 2, rows, half)
    grad_hidden = jnp.sum(shares.astype(jnp.float32), axis=0).transpose(1, 0, 2).reshape(rows, block)
    return (ce_loss, z_loss, grad_hidden, grad_weight)


def solution(mesh):
    placed = (P("section", "tensor"), P(("section", "tensor"), None), P(), P())
    return jax.shard_map(
        body,
        mesh=mesh,
        in_specs=placed,
        out_specs=(P(), P(), P("section", "tensor"), P(("section", "tensor"), None)),
        check_vma=False,
    )
```

```python
import functools

import jax
import jax.numpy as jnp
from jax import lax
from jax.experimental import pallas as pl
from jax.experimental.pallas import tpu as pltpu
from jax.sharding import PartitionSpec as P

z_weight = 0.0001
BOTH = ("section", "tensor")
VMEM = pl.BlockSpec(memory_space=pltpu.VMEM)
SMEM = pl.BlockSpec(memory_space=pltpu.SMEM)


def logits_kernel(core_ref, rows_ref, own_ref, pair_ref, out_ref):
    sections, tensors, rows, half = rows_ref.shape
    core = core_ref[0]
    for which, weight_ref in enumerate((own_ref, pair_ref)):
        total = jnp.zeros(out_ref.shape[1:], jnp.float32)
        for t in range(tensors):
            x = rows_ref[:, t].reshape(sections * rows, half)
            start = pl.multiple_of(t * 2 * half + core * half, half)
            total += lax.dot_general(
                weight_ref[:, pl.ds(start, half)],
                x,
                (((1,), (1,)), ((), ())),
                preferred_element_type=jnp.float32,
            )
        out_ref[which] = total


def stats_kernel(first_ref, mine_ref, other_ref, targets_ref, logits_ref, stats_ref):
    own = mine_ref[0] + other_ref[1]
    pair = mine_ref[1] + other_ref[0]
    logits_ref[0] = own
    logits_ref[1] = pair
    ids = lax.broadcasted_iota(jnp.int32, own.shape, 0) + first_ref[0]
    top = jnp.max(own, axis=0, keepdims=True)
    total = jnp.sum(jnp.exp(own - top), axis=0, keepdims=True)
    picked = jnp.sum(jnp.where(ids == targets_ref[...], own, 0.0), axis=0, keepdims=True)
    parts = [top, total, picked]
    spare = stats_ref.shape[2] - 3 * top.shape[1]
    if spare:
        parts.append(jnp.zeros((1, spare), jnp.float32))
    row = jnp.concatenate(parts, axis=1)
    stats_ref[...] = jnp.broadcast_to(row[None], stats_ref.shape)


def grads_kernel(
    place_ref, logits_ref, log_total_ref, targets_ref, mask_ref, own_ref, pair_ref, dlogits_ref, out_ref
):
    sections, tensors, rows, half = out_ref.shape
    core = place_ref[0]
    log_total = log_total_ref[...]
    kept = mask_ref[...].astype(jnp.float32)
    factor = 1.0 + 2.0 * z_weight * log_total
    turned = []
    for which in range(2):
        probs = jnp.exp(logits_ref[which] - log_total)
        ids = lax.broadcasted_iota(jnp.int32, probs.shape, 0) + place_ref[1 + which]
        hit = (ids == targets_ref[...]).astype(jnp.float32)
        dlogits = kept * (factor * probs - hit)
        if which == 0:
            dlogits_ref[...] = dlogits.astype(jnp.bfloat16)
        turned.append(dlogits.T.astype(jnp.bfloat16))
    for t in range(tensors):
        start = pl.multiple_of(t * 2 * half + core * half, half)
        part = jnp.dot(turned[0], own_ref[:, pl.ds(start, half)], preferred_element_type=jnp.float32)
        part += jnp.dot(turned[1], pair_ref[:, pl.ds(start, half)], preferred_element_type=jnp.float32)
        out_ref[:, t] = part.reshape(sections, rows, half).astype(jnp.bfloat16)


def weight_kernel(core_ref, dlogits_ref, mine_ref, other_ref, out_ref):
    sections, _, rows, half = mine_ref.shape
    core = core_ref[0]
    for ref, place in ((mine_ref, core), (other_ref, 1 - core)):
        x = ref[:, 0].reshape(sections * rows, half)
        out_ref[:, pl.ds(pl.multiple_of(place * half, half), half)] = jnp.dot(
            dlogits_ref[...], x, preferred_element_type=jnp.float32
        ).astype(jnp.bfloat16)


def body(hidden, out_weight, targets, token_mask):
    sections, tensors = lax.axis_size("section"), lax.axis_size("tensor")
    devices = sections * tensors
    vocab_dev, width = out_weight.shape
    rows, block = hidden.shape
    half = block // 2
    tokens = sections * rows
    f32, bf16 = jnp.float32, jnp.bfloat16
    tensor = lax.axis_index("tensor")
    core = (tensor % 2).astype(jnp.int32)
    index = (lax.axis_index("section") * tensors + tensor).astype(jnp.int32)
    first = index * vocab_dev
    pair_first = first + (1 - 2 * core) * vocab_dev
    swap = [(i, i ^ 1) for i in range(tensors)]
    target_row = targets.reshape(1, tokens)
    mask_row = token_mask.reshape(1, tokens)

    pair_weight = lax.ppermute(out_weight, "tensor", swap)
    halves = hidden.reshape(rows, 2, half).transpose(1, 0, 2)
    sent = jnp.broadcast_to(halves[None], (devices // 2, 2, rows, half)).reshape(devices, rows, half)
    mine = lax.all_to_all(sent, BOTH, 0, 0).reshape(sections, tensors, rows, half)
    other = lax.ppermute(mine, "tensor", swap)

    flops = 2 * tokens * 2 * vocab_dev * width // 2
    partial = pl.pallas_call(
        logits_kernel,
        out_shape=jax.ShapeDtypeStruct((2, vocab_dev, tokens), f32),
        in_specs=[SMEM, VMEM, VMEM, VMEM],
        out_specs=VMEM,
        cost_estimate=pl.CostEstimate(flops=flops, bytes_accessed=2 * vocab_dev * width, transcendentals=0),
        name="half_logits",
    )(core[None], mine, out_weight, pair_weight)
    partial_other = lax.ppermute(partial, "tensor", swap)

    lanes = -(-3 * tokens // 128) * 128
    logits, stats = pl.pallas_call(
        stats_kernel,
        out_shape=(
            jax.ShapeDtypeStruct((2, vocab_dev, tokens), f32),
            jax.ShapeDtypeStruct((devices, 1, lanes), f32),
        ),
        in_specs=[SMEM, VMEM, VMEM, VMEM],
        out_specs=(VMEM, VMEM),
        cost_estimate=pl.CostEstimate(
            flops=8 * vocab_dev * tokens, bytes_accessed=24 * vocab_dev * tokens, transcendentals=vocab_dev * tokens
        ),
        name="row_stats",
    )(first[None], partial, partial_other, target_row)

    stats = lax.all_to_all(stats, BOTH, 0, 0).reshape(devices, lanes)
    tops = stats[:, :tokens]
    totals = stats[:, tokens : 2 * tokens]
    picked = jnp.sum(stats[:, 2 * tokens : 3 * tokens], axis=0)
    row_top = jnp.max(tops, axis=0)
    row_total = jnp.sum(totals * jnp.exp(tops - row_top[None, :]), axis=0)
    log_total = row_top + jnp.log(row_total)
    kept = token_mask.astype(f32)
    ce_loss = jnp.sum(kept * (log_total - picked)) / tokens
    z_loss = jnp.sum(kept * log_total * log_total) / tokens

    dlogits, parts = pl.pallas_call(
        grads_kernel,
        out_shape=(
            jax.ShapeDtypeStruct((vocab_dev, tokens), bf16),
            jax.ShapeDtypeStruct((sections, tensors, rows, half), bf16),
        ),
        in_specs=[SMEM, VMEM, VMEM, VMEM, VMEM, VMEM, VMEM],
        out_specs=(VMEM, VMEM),
        cost_estimate=pl.CostEstimate(
            flops=flops, bytes_accessed=2 * vocab_dev * width, transcendentals=2 * vocab_dev * tokens
        ),
        name="grad_parts",
    )(
        jnp.stack([core, first, pair_first]),
        logits,
        log_total.reshape(1, tokens),
        target_row,
        mask_row,
        out_weight,
        pair_weight,
    )
    shares = lax.all_to_all(parts.reshape(devices, rows, half), BOTH, 0, 0)

    grad_weight = pl.pallas_call(
        weight_kernel,
        out_shape=jax.ShapeDtypeStruct((vocab_dev, width), bf16),
        grid=(tensors,),
        in_specs=[
            SMEM,
            pl.BlockSpec((vocab_dev, tokens), lambda t: (0, 0)),
            pl.BlockSpec((sections, 1, rows, half), lambda t: (0, t, 0, 0)),
            pl.BlockSpec((sections, 1, rows, half), lambda t: (0, t, 0, 0)),
        ],
        out_specs=pl.BlockSpec((vocab_dev, block), lambda t: (0, t)),
        cost_estimate=pl.CostEstimate(
            flops=2 * tokens * vocab_dev * width,
            bytes_accessed=2 * vocab_dev * width + 2 * tokens * width,
            transcendentals=0,
        ),
        name="grad_weight",
    )(core[None], dlogits, mine, other)

    shares = shares.reshape(devices // 2, 2, rows, half)
    grad_hidden = jnp.sum(shares.astype(f32), axis=0).transpose(1, 0, 2).reshape(rows, block)
    return (ce_loss, z_loss, grad_hidden, grad_weight)


def solution(mesh):
    placed = (P("section", "tensor"), P(("section", "tensor"), None), P(), P())
    return jax.shard_map(
        body,
        mesh=mesh,
        in_specs=placed,
        out_specs=(P(), P(), P("section", "tensor"), P(("section", "tensor"), None)),
        check_vma=False,
    )
```

```python
import functools

import jax
import jax.numpy as jnp
from jax import lax
from jax.experimental import pallas as pl
from jax.experimental.pallas import tpu as pltpu
from jax.sharding import PartitionSpec as P


z_weight = 0.0001
BOTH = ("section", "tensor")
VMEM = pl.BlockSpec(memory_space=pltpu.VMEM)
SMEM = pl.BlockSpec(memory_space=pltpu.SMEM)
SMALL = pltpu.CompilerParams(vmem_limit_bytes=16 << 20)


def split_kernel(half, place_ref, weight_ref, keep_ref, give_ref):
    core = place_ref[0]
    for t in range(keep_ref.shape[1] // half):
        for ref, place in ((keep_ref, core), (give_ref, 1 - core)):
            start = pl.multiple_of((2 * t + place) * half, half)
            ref[:, t * half : (t + 1) * half] = weight_ref[:, pl.ds(start, half)]


def logits_kernel(rows_ref, own_ref, pair_ref, out_ref):
    sections, tensors, rows, half = rows_ref.shape
    for which, weight_ref in enumerate((own_ref, pair_ref)):
        total = jnp.zeros(out_ref.shape[1:], jnp.float32)
        for t in range(tensors):
            x = rows_ref[:, t].reshape(sections * rows, half)
            total += lax.dot_general(
                weight_ref[:, t * half : (t + 1) * half],
                x,
                (((1,), (1,)), ((), ())),
                preferred_element_type=jnp.float32,
            )
        out_ref[which] = total


def stats_kernel(place_ref, mine_ref, other_ref, targets_ref, logits_ref, stats_ref):
    own = mine_ref[0] + other_ref[1]
    pair = mine_ref[1] + other_ref[0]
    logits_ref[0] = own
    logits_ref[1] = pair
    ids = lax.broadcasted_iota(jnp.int32, own.shape, 0) + place_ref[1]
    top = jnp.max(own, axis=0, keepdims=True)
    total = jnp.sum(jnp.exp(own - top), axis=0, keepdims=True)
    picked = jnp.sum(jnp.where(ids == targets_ref[...], own, 0.0), axis=0, keepdims=True)
    parts = [top, total, picked]
    spare = stats_ref.shape[2] - 3 * top.shape[1]
    if spare:
        parts.append(jnp.zeros((1, spare), jnp.float32))
    row = jnp.concatenate(parts, axis=1)
    stats_ref[...] = jnp.broadcast_to(row[None], stats_ref.shape)


def grads_kernel(
    place_ref, logits_ref, log_total_ref, targets_ref, mask_ref, own_ref, pair_ref, dlogits_ref, out_ref, kept_ref
):
    sections, tensors, rows, half = out_ref.shape
    log_total = log_total_ref[...]
    kept_ref[...] = log_total
    kept = mask_ref[...].astype(jnp.float32)
    factor = 1.0 + 2.0 * z_weight * log_total
    turned = []
    for which in range(2):
        probs = jnp.exp(logits_ref[which] - log_total)
        ids = lax.broadcasted_iota(jnp.int32, probs.shape, 0) + place_ref[1 + which]
        hit = (ids == targets_ref[...]).astype(jnp.float32)
        dlogits = kept * (factor * probs - hit)
        if which == 0:
            dlogits_ref[...] = dlogits.astype(jnp.bfloat16)
        turned.append(dlogits.T.astype(jnp.bfloat16))
    for t in range(tensors):
        columns = slice(t * half, (t + 1) * half)
        part = jnp.dot(turned[0], own_ref[:, columns], preferred_element_type=jnp.float32)
        part += jnp.dot(turned[1], pair_ref[:, columns], preferred_element_type=jnp.float32)
        out_ref[:, t] = part.reshape(sections, rows, half).astype(jnp.bfloat16)


def weight_kernel(place_ref, dlogits_ref, mine_ref, other_ref, out_ref):
    sections, _, rows, half = mine_ref.shape
    core = place_ref[0]
    for ref, place in ((mine_ref, core), (other_ref, 1 - core)):
        x = ref[:, 0].reshape(sections * rows, half)
        out_ref[:, pl.ds(pl.multiple_of(place * half, half), half)] = jnp.dot(
            dlogits_ref[...], x, preferred_element_type=jnp.float32
        ).astype(jnp.bfloat16)


def body(hidden, out_weight, targets, token_mask):
    sections, tensors = lax.axis_size("section"), lax.axis_size("tensor")
    devices = sections * tensors
    vocab_dev, width = out_weight.shape
    rows, block = hidden.shape
    half = block // 2
    tokens = sections * rows
    f32, bf16 = jnp.float32, jnp.bfloat16
    tensor = lax.axis_index("tensor")
    core = (tensor % 2).astype(jnp.int32)
    first = (lax.axis_index("section") * tensors + tensor).astype(jnp.int32) * vocab_dev
    place = jnp.stack([core, first, first + (1 - 2 * core) * vocab_dev])
    swap = [(i, i ^ 1) for i in range(tensors)]
    target_row = targets.reshape(1, tokens)
    mask_row = token_mask.reshape(1, tokens)

    halves = hidden.reshape(rows, 2, half).transpose(1, 0, 2)
    sent = jnp.broadcast_to(halves[None], (devices // 2, 2, rows, half)).reshape(devices, rows, half)
    mine = lax.all_to_all(sent, BOTH, 0, 0)
    mine = mine.reshape(sections, tensors, rows, half)
    other = lax.ppermute(mine, "tensor", swap)

    half_weight = jax.ShapeDtypeStruct((vocab_dev, width // 2), bf16)
    own_weight, given = pl.pallas_call(
        functools.partial(split_kernel, half),
        out_shape=(half_weight, half_weight),
        in_specs=[SMEM, VMEM],
        out_specs=(VMEM, VMEM),
        compiler_params=SMALL,
        cost_estimate=pl.CostEstimate(flops=0, bytes_accessed=4 * vocab_dev * width, transcendentals=0),
        name="split_weight",
    )(place, out_weight)
    pair_weight = lax.ppermute(given, "tensor", swap)

    flops = 2 * tokens * vocab_dev * width
    partial = pl.pallas_call(
        logits_kernel,
        out_shape=jax.ShapeDtypeStruct((2, vocab_dev, tokens), f32),
        in_specs=[VMEM, VMEM, VMEM],
        out_specs=VMEM,
        compiler_params=SMALL,
        cost_estimate=pl.CostEstimate(flops=flops, bytes_accessed=2 * vocab_dev * width, transcendentals=0),
        name="half_logits",
    )(mine, own_weight, pair_weight)
    partial_other = lax.ppermute(partial, "tensor", swap)

    lanes = -(-3 * tokens // 128) * 128
    logits, stats = pl.pallas_call(
        stats_kernel,
        out_shape=(
            jax.ShapeDtypeStruct((2, vocab_dev, tokens), f32),
            jax.ShapeDtypeStruct((devices, 1, lanes), f32),
        ),
        in_specs=[SMEM, VMEM, VMEM, VMEM],
        out_specs=(VMEM, VMEM),
        compiler_params=SMALL,
        cost_estimate=pl.CostEstimate(
            flops=8 * vocab_dev * tokens, bytes_accessed=24 * vocab_dev * tokens, transcendentals=vocab_dev * tokens
        ),
        name="row_stats",
    )(place, partial, partial_other, target_row)

    stats = lax.all_to_all(stats, BOTH, 0, 0).reshape(devices, lanes)
    tops = stats[:, :tokens]
    totals = stats[:, tokens : 2 * tokens]
    row_top = jnp.max(tops, axis=0)
    row_total = jnp.sum(totals * jnp.exp(tops - row_top[None, :]), axis=0)
    log_total = row_top + jnp.log(row_total)

    dlogits, parts, log_total = pl.pallas_call(
        grads_kernel,
        out_shape=(
            jax.ShapeDtypeStruct((vocab_dev, tokens), bf16),
            jax.ShapeDtypeStruct((sections, tensors, rows, half), bf16),
            jax.ShapeDtypeStruct((1, tokens), f32),
        ),
        in_specs=[SMEM, VMEM, VMEM, VMEM, VMEM, VMEM, VMEM],
        out_specs=(VMEM, VMEM, VMEM),
        compiler_params=SMALL,
        cost_estimate=pl.CostEstimate(
            flops=flops, bytes_accessed=2 * vocab_dev * width, transcendentals=2 * vocab_dev * tokens
        ),
        name="grad_parts",
    )(place, logits, log_total.reshape(1, tokens), target_row, mask_row, own_weight, pair_weight)
    shares = lax.all_to_all(parts.reshape(devices, rows, half), BOTH, 0, 0)

    log_total = log_total.reshape(tokens)
    picked = jnp.sum(stats[:, 2 * tokens : 3 * tokens], axis=0)
    kept = token_mask.astype(f32)
    ce_loss = jnp.sum(kept * (log_total - picked)) / tokens
    z_loss = jnp.sum(kept * log_total * log_total) / tokens

    grad_weight = pl.pallas_call(
        weight_kernel,
        out_shape=jax.ShapeDtypeStruct((vocab_dev, width), bf16),
        grid=(tensors,),
        in_specs=[
            SMEM,
            pl.BlockSpec((vocab_dev, tokens), lambda t: (0, 0)),
            pl.BlockSpec((sections, 1, rows, half), lambda t: (0, t, 0, 0)),
            pl.BlockSpec((sections, 1, rows, half), lambda t: (0, t, 0, 0)),
        ],
        out_specs=pl.BlockSpec((vocab_dev, block), lambda t: (0, t)),
        compiler_params=SMALL,
        cost_estimate=pl.CostEstimate(
            flops=flops, bytes_accessed=2 * vocab_dev * width + 2 * tokens * width, transcendentals=0
        ),
        name="grad_weight",
    )(place, dlogits, mine, other)

    shares = shares.reshape(devices // 2, 2, rows, half)
    grad_hidden = jnp.sum(shares.astype(f32), axis=0).transpose(1, 0, 2).reshape(rows, block)
    return (ce_loss, z_loss, grad_hidden, grad_weight)


def solution(mesh):
    placed = (P("section", "tensor"), P(("section", "tensor"), None), P(), P())
    return jax.shard_map(
        body,
        mesh=mesh,
        in_specs=placed,
        out_specs=(P(), P(), P("section", "tensor"), P(("section", "tensor"), None)),
        check_vma=False,
    )
```

```python
import jax
import jax.numpy as jnp
from jax import lax
from jax.experimental import pallas as pl
from jax.experimental.pallas import tpu as pltpu
from jax.sharding import PartitionSpec as P


z_weight = 0.0001
BOTH = ("section", "tensor")
VMEM = pl.BlockSpec(memory_space=pltpu.VMEM)
HBM = pl.BlockSpec(memory_space=pltpu.HBM)
DMA = pltpu.SemaphoreType.DMA
SMALL = pltpu.CompilerParams(vmem_limit_bytes=16 << 20)


def this_core():
    return lax.rem(lax.axis_index("tensor"), 2)


def half_columns(block, core, half):
    return pl.ds(pl.multiple_of((2 * block + core) * half, half), half)


def first_entry(vocab_dev, other):
    index = lax.axis_index("section") * lax.axis_size("tensor") + lax.axis_index("tensor")
    if other:
        index = index + 1 - 2 * this_core()
    return index * vocab_dev


def spread_kernel(hidden_ref, out_ref):
    half = out_ref.shape[2]
    for device in range(out_ref.shape[0]):
        part = device % 2
        out_ref[device] = hidden_ref[:, part * half : (part + 1) * half]


def logits_kernel(rows_ref, weight_ref, out_ref):
    sections, tensors, rows, half = rows_ref.shape
    total = jnp.zeros(out_ref.shape, jnp.float32)
    for t in range(tensors):
        x = rows_ref[:, t].reshape(sections * rows, half)
        columns = half_columns(t, this_core(), half)
        total += lax.dot_general(
            weight_ref[:, columns], x, (((1,), (1,)), ((), ())), preferred_element_type=jnp.float32
        )
    out_ref[...] = total


def stats_kernel(mine_ref, other_ref, targets_ref, logits_ref, stats_ref):
    own = mine_ref[...] + other_ref[...]
    logits_ref[...] = own
    ids = lax.broadcasted_iota(jnp.int32, own.shape, 0) + first_entry(own.shape[0], False)
    top = jnp.max(own, axis=0, keepdims=True)
    total = jnp.sum(jnp.exp(own - top), axis=0, keepdims=True)
    picked = jnp.sum(jnp.where(ids == targets_ref[...], own, 0.0), axis=0, keepdims=True)
    parts = [top, total, picked]
    spare = stats_ref.shape[2] - 3 * top.shape[1]
    if spare:
        parts.append(jnp.zeros((1, spare), jnp.float32))
    row = jnp.concatenate(parts, axis=1)
    stats_ref[...] = jnp.broadcast_to(row[None], stats_ref.shape)


def grads_kernel(
    own_logits_ref,
    pair_logits_ref,
    log_total_ref,
    targets_ref,
    mask_ref,
    own_ref,
    pair_ref,
    dlogits_ref,
    out_ref,
    parts_ref,
    sems,
):
    sections, tensors, rows, half = out_ref.shape
    vocab_dev = own_ref.shape[0]
    core = this_core()
    log_total = log_total_ref[...]
    kept = mask_ref[...].astype(jnp.float32)
    factor = 1.0 + 2.0 * z_weight * log_total
    turned = []
    for ref, other in ((own_logits_ref, False), (pair_logits_ref, True)):
        probs = jnp.exp(ref[...] - log_total)
        ids = lax.broadcasted_iota(jnp.int32, probs.shape, 0) + first_entry(vocab_dev, other)
        hit = (ids == targets_ref[...]).astype(jnp.float32)
        dlogits = kept * (factor * probs - hit)
        if not other:
            dlogits_ref[...] = dlogits.astype(jnp.bfloat16)
        turned.append(dlogits.T.astype(jnp.bfloat16))
    copies = []
    for t in range(tensors):
        columns = half_columns(t, core, half)
        part = jnp.dot(turned[0], own_ref[:, columns], preferred_element_type=jnp.float32)
        part += jnp.dot(turned[1], pair_ref[:, columns], preferred_element_type=jnp.float32)
        parts_ref[:, t] = part.reshape(sections, rows, half).astype(jnp.bfloat16)
        copies.append(pltpu.make_async_copy(parts_ref.at[:, t], out_ref.at[:, t], sems.at[t]))
        copies[-1].start()
    for copy in copies:
        copy.wait()


def weight_kernel(
    dlogits_ref, mine_ref, other_ref, log_total_ref, picked_ref, mask_ref, out_ref, ce_ref, z_ref, blocks_ref, sems
):
    sections, tensors, rows, half = mine_ref.shape
    tokens = sections * rows
    core = this_core()
    copies = []
    for t in range(tensors):
        for ref, place in ((mine_ref, core), (other_ref, 1 - core)):
            x = ref[:, t].reshape(tokens, half)
            blocks_ref[:, half_columns(t, place, half)] = jnp.dot(
                dlogits_ref[...], x, preferred_element_type=jnp.float32
            ).astype(jnp.bfloat16)
        columns = slice(2 * t * half, 2 * (t + 1) * half)
        copies.append(pltpu.make_async_copy(blocks_ref.at[:, columns], out_ref.at[:, columns], sems.at[t]))
        copies[-1].start()
    log_total = log_total_ref[...]
    kept = mask_ref[...].astype(jnp.float32)
    ce_ref[...] = jnp.sum(kept * (log_total - picked_ref[...]), axis=1, keepdims=True) / tokens
    z_ref[...] = jnp.sum(kept * log_total * log_total, axis=1, keepdims=True) / tokens
    for copy in copies:
        copy.wait()


def body(hidden, out_weight, targets, token_mask):
    sections, tensors = lax.axis_size("section"), lax.axis_size("tensor")
    devices = sections * tensors
    vocab_dev, width = out_weight.shape
    rows, block = hidden.shape
    half = block // 2
    tokens = sections * rows
    f32, bf16 = jnp.float32, jnp.bfloat16
    swap = [(i, i ^ 1) for i in range(tensors)]
    target_row = targets.reshape(1, tokens)
    mask_row = token_mask.reshape(1, tokens)
    flops = 2 * tokens * vocab_dev * width

    pair_weight = lax.ppermute(out_weight, "tensor", swap)

    sent = pl.pallas_call(
        spread_kernel,
        out_shape=jax.ShapeDtypeStruct((devices, rows, half), bf16),
        in_specs=[VMEM],
        out_specs=VMEM,
        compiler_params=SMALL,
        name="spread_rows",
    )(hidden)
    mine = lax.all_to_all(sent, BOTH, 0, 0)
    mine = mine.reshape(sections, tensors, rows, half)
    other = lax.ppermute(mine, "tensor", swap)

    half_logits = pl.pallas_call(
        logits_kernel,
        out_shape=jax.ShapeDtypeStruct((vocab_dev, tokens), f32),
        in_specs=[VMEM, VMEM],
        out_specs=VMEM,
        compiler_params=SMALL,
        cost_estimate=pl.CostEstimate(flops=flops // 2, bytes_accessed=vocab_dev * width, transcendentals=0),
        name="half_logits",
    )
    traded = lax.ppermute(half_logits(mine, pair_weight), "tensor", swap)
    own_part = half_logits(mine, out_weight)

    lanes = -(-3 * tokens // 128) * 128
    own_logits, stats = pl.pallas_call(
        stats_kernel,
        out_shape=(
            jax.ShapeDtypeStruct((vocab_dev, tokens), f32),
            jax.ShapeDtypeStruct((devices, 1, lanes), f32),
        ),
        in_specs=[VMEM, VMEM, VMEM],
        out_specs=(VMEM, VMEM),
        compiler_params=SMALL,
        cost_estimate=pl.CostEstimate(
            flops=8 * vocab_dev * tokens, bytes_accessed=16 * vocab_dev * tokens, transcendentals=vocab_dev * tokens
        ),
        name="row_stats",
    )(own_part, traded, target_row)
    pair_logits = lax.ppermute(own_logits, "tensor", swap)

    stats = lax.all_to_all(stats, BOTH, 0, 0)
    stats = stats.reshape(devices, lanes)
    tops = stats[:, :tokens]
    totals = stats[:, tokens : 2 * tokens]
    row_top = jnp.max(tops, axis=0)
    row_total = jnp.sum(totals * jnp.exp(tops - row_top[None, :]), axis=0)
    log_total = (row_top + jnp.log(row_total)).reshape(1, tokens)
    picked = jnp.sum(stats[:, 2 * tokens : 3 * tokens], axis=0).reshape(1, tokens)

    dlogits, parts = pl.pallas_call(
        grads_kernel,
        out_shape=(
            jax.ShapeDtypeStruct((vocab_dev, tokens), bf16),
            jax.ShapeDtypeStruct((sections, tensors, rows, half), bf16),
        ),
        in_specs=[VMEM] * 7,
        out_specs=(VMEM, HBM),
        scratch_shapes=[pltpu.VMEM((sections, tensors, rows, half), bf16), DMA((tensors,))],
        compiler_params=SMALL,
        cost_estimate=pl.CostEstimate(
            flops=flops, bytes_accessed=2 * vocab_dev * width, transcendentals=2 * vocab_dev * tokens
        ),
        name="grad_parts",
    )(own_logits, pair_logits, log_total, target_row, mask_row, out_weight, pair_weight)
    shares = lax.all_to_all(parts.reshape(devices, rows, half), BOTH, 0, 0)

    scalar = jax.ShapeDtypeStruct((1, 1), f32)
    grad_weight, ce_loss, z_loss = pl.pallas_call(
        weight_kernel,
        out_shape=(jax.ShapeDtypeStruct((vocab_dev, width), bf16), scalar, scalar),
        in_specs=[VMEM] * 6,
        out_specs=(HBM, VMEM, VMEM),
        scratch_shapes=[pltpu.VMEM((vocab_dev, width), bf16), DMA((tensors,))],
        compiler_params=SMALL,
        cost_estimate=pl.CostEstimate(
            flops=flops, bytes_accessed=2 * vocab_dev * width + 2 * tokens * width, transcendentals=0
        ),
        name="grad_weight",
    )(dlogits, mine, other, log_total, picked, mask_row)

    shares = shares.reshape(devices // 2, 2, rows, half)
    grad_hidden = jnp.sum(shares.astype(f32), axis=0).transpose(1, 0, 2).reshape(rows, block)
    return (ce_loss.reshape(()), z_loss.reshape(()), grad_hidden, grad_weight)


def solution(mesh):
    placed = (P("section", "tensor"), P(("section", "tensor"), None), P(), P())
    return jax.shard_map(
        body,
        mesh=mesh,
        in_specs=placed,
        out_specs=(P(), P(), P("section", "tensor"), P(("section", "tensor"), None)),
        check_vma=False,
    )
```

```python
import jax
import jax.numpy as jnp
from jax import lax
from jax.experimental import pallas as pl
from jax.experimental.pallas import tpu as pltpu
from jax.sharding import PartitionSpec as P


z_weight = 0.0001
BOTH = ("section", "tensor")
LANES = 128
VMEM = pl.BlockSpec(memory_space=pltpu.VMEM)
HBM = pl.BlockSpec(memory_space=pltpu.HBM)
DMA = pltpu.SemaphoreType.DMA
SMALL = pltpu.CompilerParams(vmem_limit_bytes=16 << 20)
F32, BF16 = jnp.float32, jnp.bfloat16


def tiles_of(count):
    return -(-count // LANES)


def this_core():
    return lax.rem(lax.axis_index("tensor"), 2)


def half_columns(block, core, half):
    return pl.ds(pl.multiple_of((2 * block + core) * half, half), half)


def target_hits(shape, targets, other):
    index = lax.axis_index("section") * lax.axis_size("tensor") + lax.axis_index("tensor")
    if other:
        index = index + 1 - 2 * this_core()
    return lax.broadcasted_iota(jnp.int32, shape, 0) + index * shape[0] == targets


def spread_kernel(hidden_ref, out_ref):
    half = out_ref.shape[2]
    for device in range(out_ref.shape[0]):
        part = device % 2
        out_ref[device] = hidden_ref[:, part * half : (part + 1) * half]


def logits_kernel(rows_ref, weight_ref, out_ref):
    sections, tensors, rows, half = rows_ref.shape
    core = this_core()
    total = jnp.zeros(out_ref.shape, F32)
    for t in range(tensors):
        x = rows_ref[:, t].reshape(sections * rows, half)
        total += lax.dot_general(
            weight_ref[:, half_columns(t, core, half)], x, (((1,), (1,)), ((), ())), preferred_element_type=F32
        )
    out_ref[...] = total


def parts_kernel(
    own_mine_ref, own_other_ref, pair_mine_ref, pair_other_ref, targets_ref, own_ref, pair_ref, logits_ref, out_ref
):
    vocab_dev, tokens = own_mine_ref.shape
    sections, tensors, _, rows, _ = out_ref.shape
    half = own_ref.shape[1] // tensors // 2
    pieces = half // LANES
    core = this_core()
    targets = targets_ref[...]
    logits = (own_mine_ref[...] + own_other_ref[...], pair_mine_ref[...] + pair_other_ref[...])
    logits_ref[...] = logits[0]
    hits = [target_hits((vocab_dev, tokens), targets, other) for other in (False, True)]
    rest = [jnp.where(hit, -jnp.inf, x) for hit, x in zip(hits, logits)]
    top = jnp.maximum(*[jnp.max(x, axis=0, keepdims=True) for x in rest])
    shares = [jnp.exp(x - top) for x in rest]
    total = sum(jnp.sum(x, axis=0, keepdims=True) for x in shares)
    picked = sum(jnp.sum(jnp.where(hit, x, 0.0), axis=0, keepdims=True) for hit, x in zip(hits, logits))

    turned = []
    for share, hit in zip(shares, hits):
        share = share.T
        coarse = share.astype(BF16)
        fine = (share - coarse.astype(F32)).astype(BF16)
        turned.append(jnp.concatenate([coarse, fine, hit.astype(F32).T.astype(BF16)], axis=0))
    for t in range(tensors):
        columns = half_columns(t, core, half)
        part = jnp.dot(turned[0], own_ref[:, columns], preferred_element_type=F32)
        part += jnp.dot(turned[1], pair_ref[:, columns], preferred_element_type=F32)
        weighted = (part[:tokens] + part[tokens : 2 * tokens]).reshape(sections, rows, half).astype(BF16)
        targeted = part[2 * tokens :].reshape(sections, rows, half).astype(BF16)
        for j in range(pieces):
            lanes = slice(j * LANES, (j + 1) * LANES)
            out_ref[:, t, j] = weighted[:, :, lanes]
            out_ref[:, t, pieces + j] = targeted[:, :, lanes]

    spare = tiles_of(3 * tokens) * LANES - 3 * tokens
    row = [top, total, picked] + ([jnp.zeros((1, spare), F32)] if spare else [])
    row = jnp.concatenate(row, axis=1)
    digits = []
    for _ in range(3):
        digits.append(row.astype(BF16).astype(F32))
        row = row - digits[-1]
    digits.append(jnp.zeros((rows - 3, row.shape[1]), F32))
    digits = jnp.concatenate(digits, axis=0).astype(BF16)
    for j in range(tiles_of(3 * tokens)):
        tile = digits[:, j * LANES : (j + 1) * LANES]
        for t in range(tensors):
            out_ref[:, t, 2 * pieces + j] = jnp.broadcast_to(tile[None], (sections, rows, LANES))


def totals_kernel(
    parts_ref, logits_ref, targets_ref, mask_ref, dlogits_ref, scales_ref, log_total_ref, picked_ref, table_ref
):
    chips = table_ref.shape[0]
    tokens = log_total_ref.shape[1]
    first = parts_ref.shape[1] - tiles_of(3 * tokens)
    for k in range(chips):
        for j in range(tiles_of(3 * tokens)):
            tile = parts_ref[2 * k, first + j].astype(F32)
            table_ref[k : k + 1, j * LANES : (j + 1) * LANES] = jnp.sum(tile, axis=0, keepdims=True)
    table = table_ref[...]
    tops = table[:, :tokens]
    totals = table[:, tokens : 2 * tokens]
    picked = jnp.sum(table[:, 2 * tokens : 3 * tokens], axis=0, keepdims=True)
    row_top = jnp.maximum(jnp.max(tops, axis=0, keepdims=True), picked)
    row_total = jnp.sum(totals * jnp.exp(tops - row_top), axis=0, keepdims=True) + jnp.exp(picked - row_top)
    log_total = row_top + jnp.log(row_total)
    kept = mask_ref[...].astype(F32)
    factor = 1.0 + 2.0 * z_weight * log_total
    hit = target_hits(logits_ref.shape, targets_ref[...], False).astype(F32)
    dlogits_ref[...] = (kept * (factor * jnp.exp(logits_ref[...] - log_total) - hit)).astype(BF16)
    log_total_ref[...] = log_total
    picked_ref[...] = picked

    scales = (kept * (factor * jnp.exp(tops - log_total))).astype(BF16).astype(F32)
    scale = (kept * (factor * jnp.exp(picked - log_total) - 1.0)).astype(BF16).astype(F32)
    spare = scales_ref.shape[1] - chips - 1
    scales_ref[...] = jnp.concatenate([scales, scale, jnp.zeros((spare, tokens), F32)], axis=0).T


def finish_kernel(
    dlogits_ref,
    mine_ref,
    other_ref,
    parts_ref,
    scales_ref,
    log_total_ref,
    picked_ref,
    mask_ref,
    weight_grad_ref,
    hidden_grad_ref,
    ce_ref,
    z_ref,
    blocks_ref,
    sems,
):
    sections, tensors, rows, half = mine_ref.shape
    tokens = sections * rows
    chips = sections * tensors // 2
    pieces = half // LANES
    core = this_core()
    dlogits = dlogits_ref[...]
    copies = []
    for t in range(tensors):
        for ref, place in ((mine_ref, core), (other_ref, 1 - core)):
            x = ref[:, t].reshape(tokens, half)
            blocks_ref[:, half_columns(t, place, half)] = jnp.dot(
                dlogits, x, preferred_element_type=F32
            ).astype(BF16)
        columns = slice(2 * t * half, 2 * (t + 1) * half)
        copies.append(pltpu.make_async_copy(blocks_ref.at[:, columns], weight_grad_ref.at[:, columns], sems.at[t]))
        copies[-1].start()

    here = scales_ref[pl.ds(pl.multiple_of(lax.axis_index("section") * rows, rows), rows), :]
    for part in range(2):
        for j in range(pieces):
            weighted = jnp.zeros((rows, LANES), F32)
            targeted = jnp.zeros((rows, LANES), F32)
            for k in range(chips):
                weighted += here[:, k : k + 1] * parts_ref[2 * k + part, j].astype(F32)
                targeted += parts_ref[2 * k + part, pieces + j].astype(F32)
            start = part * half + j * LANES
            hidden_grad_ref[:, start : start + LANES] = weighted + here[:, chips : chips + 1] * targeted

    log_total = log_total_ref[...]
    kept = mask_ref[...].astype(F32)
    ce_ref[...] = jnp.sum(kept * (log_total - picked_ref[...]), axis=1, keepdims=True) / tokens
    z_ref[...] = jnp.sum(kept * log_total * log_total, axis=1, keepdims=True) / tokens
    for copy in copies:
        copy.wait()


def body(hidden, out_weight, targets, token_mask):
    sections, tensors = lax.axis_size("section"), lax.axis_size("tensor")
    devices = sections * tensors
    vocab_dev, width = out_weight.shape
    rows, block = hidden.shape
    half = block // 2
    tokens = sections * rows
    swap = [(i, i ^ 1) for i in range(tensors)]
    target_row = targets.reshape(1, tokens)
    mask_row = token_mask.reshape(1, tokens)
    flops = 2 * tokens * vocab_dev * width
    tiles = 2 * (half // LANES) + tiles_of(3 * tokens)

    pair_weight = lax.ppermute(out_weight, "tensor", swap)
    sent = pl.pallas_call(
        spread_kernel,
        out_shape=jax.ShapeDtypeStruct((devices, rows, half), BF16),
        in_specs=[VMEM],
        out_specs=VMEM,
        compiler_params=SMALL,
        name="spread_rows",
    )(hidden)
    mine = lax.all_to_all(sent, BOTH, 0, 0)
    mine = mine.reshape(sections, tensors, rows, half)

    half_logits = pl.pallas_call(
        logits_kernel,
        out_shape=jax.ShapeDtypeStruct((vocab_dev, tokens), F32),
        in_specs=[VMEM] * 2,
        out_specs=VMEM,
        compiler_params=SMALL,
        cost_estimate=pl.CostEstimate(flops=flops // 2, bytes_accessed=vocab_dev * width, transcendentals=0),
        name="half_logits",
    )
    pair_mine = half_logits(mine, pair_weight)
    own_other = lax.ppermute(pair_mine, "tensor", swap)
    own_mine = half_logits(mine, out_weight)
    pair_other = lax.ppermute(own_mine, "tensor", swap)
    other = lax.ppermute(mine, "tensor", swap)

    logits, parts = pl.pallas_call(
        parts_kernel,
        out_shape=(
            jax.ShapeDtypeStruct((vocab_dev, tokens), F32),
            jax.ShapeDtypeStruct((sections, tensors, tiles, rows, LANES), BF16),
        ),
        in_specs=[VMEM] * 7,
        out_specs=(VMEM, VMEM),
        compiler_params=SMALL,
        cost_estimate=pl.CostEstimate(
            flops=3 * flops, bytes_accessed=2 * vocab_dev * width, transcendentals=2 * vocab_dev * tokens
        ),
        name="grad_parts",
    )(own_mine, own_other, pair_mine, pair_other, target_row, out_weight, pair_weight)
    parts = lax.all_to_all(parts.reshape(devices, tiles, rows, LANES), BOTH, 0, 0)

    chips = devices // 2
    row = jax.ShapeDtypeStruct((1, tokens), F32)
    dlogits, scales, log_total, picked = pl.pallas_call(
        totals_kernel,
        out_shape=(
            jax.ShapeDtypeStruct((vocab_dev, tokens), BF16),
            jax.ShapeDtypeStruct((tokens, tiles_of(chips + 1) * LANES), F32),
            row,
            row,
        ),
        in_specs=[VMEM] * 4,
        out_specs=(VMEM,) * 4,
        scratch_shapes=[pltpu.VMEM((chips, tiles_of(3 * tokens) * LANES), F32)],
        compiler_params=SMALL,
        cost_estimate=pl.CostEstimate(
            flops=8 * vocab_dev * tokens, bytes_accessed=16 * vocab_dev * tokens, transcendentals=vocab_dev * tokens
        ),
        name="totals",
    )(parts, logits, target_row, mask_row)

    scalar = jax.ShapeDtypeStruct((1, 1), F32)
    grad_weight, grad_hidden, ce_loss, z_loss = pl.pallas_call(
        finish_kernel,
        out_shape=(
            jax.ShapeDtypeStruct((vocab_dev, width), BF16),
            jax.ShapeDtypeStruct((rows, block), F32),
            scalar,
            scalar,
        ),
        in_specs=[VMEM] * 8,
        out_specs=(HBM, VMEM, VMEM, VMEM),
        scratch_shapes=[pltpu.VMEM((vocab_dev, width), BF16), DMA((tensors,))],
        compiler_params=SMALL,
        cost_estimate=pl.CostEstimate(
            flops=flops, bytes_accessed=2 * vocab_dev * width + 2 * tokens * width, transcendentals=0
        ),
        name="finish",
    )(dlogits, mine, other, parts, scales, log_total, picked, mask_row)
    return (ce_loss.reshape(()), z_loss.reshape(()), grad_hidden, grad_weight)


def solution(mesh):
    placed = (P("section", "tensor"), P(("section", "tensor"), None), P(), P())
    return jax.shard_map(
        body,
        mesh=mesh,
        in_specs=placed,
        out_specs=(P(), P(), P("section", "tensor"), P(("section", "tensor"), None)),
        check_vma=False,
    )
```

```python
import jax
import jax.numpy as jnp
from jax import lax
from jax.experimental import pallas as pl
from jax.experimental.pallas import tpu as pltpu
from jax.sharding import PartitionSpec as P


z_weight = 0.0001
BOTH = ("section", "tensor")
LANES = 128
VMEM = pl.BlockSpec(memory_space=pltpu.VMEM)
HBM = pl.BlockSpec(memory_space=pltpu.HBM)
DMA = pltpu.SemaphoreType.DMA
SMALL = pltpu.CompilerParams(vmem_limit_bytes=16 << 20)
F32, BF16 = jnp.float32, jnp.bfloat16


def tiles_of(count):
    return -(-count // LANES)


def this_core():
    return lax.rem(lax.axis_index("tensor"), 2)


def half_columns(block, core, half):
    return pl.ds(pl.multiple_of((2 * block + core) * half, half), half)


def target_hits(shape, targets, other):
    index = lax.axis_index("section") * lax.axis_size("tensor") + lax.axis_index("tensor")
    if other:
        index = index + 1 - 2 * this_core()
    return lax.broadcasted_iota(jnp.int32, shape, 0) + index * shape[0] == targets


def spread_kernel(hidden_ref, out_ref):
    half = out_ref.shape[2]
    for device in range(out_ref.shape[0]):
        part = device % 2
        out_ref[device] = hidden_ref[:, part * half : (part + 1) * half]


def logits_kernel(rows_ref, weight_ref, out_ref):
    sections, tensors, rows, half = rows_ref.shape
    core = this_core()
    total = jnp.zeros(out_ref.shape, F32)
    for t in range(tensors):
        x = rows_ref[:, t].reshape(sections * rows, half)
        total += lax.dot_general(
            weight_ref[:, half_columns(t, core, half)], x, (((1,), (1,)), ((), ())), preferred_element_type=F32
        )
    out_ref[...] = total


def parts_kernel(
    own_mine_ref, own_other_ref, pair_mine_ref, pair_other_ref, targets_ref, own_ref, pair_ref, logits_ref, out_ref
):
    vocab_dev, tokens = own_mine_ref.shape
    sections, tensors, _, rows, _ = out_ref.shape
    half = own_ref.shape[1] // tensors // 2
    pieces = half // LANES
    core = this_core()
    targets = targets_ref[...]
    logits = (own_mine_ref[...] + own_other_ref[...], pair_mine_ref[...] + pair_other_ref[...])
    logits_ref[...] = logits[0]
    hits = [target_hits((vocab_dev, tokens), targets, other) for other in (False, True)]
    rest = [jnp.where(hit, -jnp.inf, x) for hit, x in zip(hits, logits)]
    top = jnp.maximum(*[jnp.max(x, axis=0, keepdims=True) for x in rest])
    shares = [jnp.exp(x - top) for x in rest]
    total = sum(jnp.sum(x, axis=0, keepdims=True) for x in shares)
    picked = sum(jnp.sum(jnp.where(hit, x, 0.0), axis=0, keepdims=True) for hit, x in zip(hits, logits))

    turned = []
    for share, hit in zip(shares, hits):
        share = share.T
        coarse = share.astype(BF16)
        fine = (share - coarse.astype(F32)).astype(BF16)
        turned.append(jnp.concatenate([coarse, fine, hit.astype(F32).T.astype(BF16)], axis=0))
    for t in range(tensors):
        columns = half_columns(t, core, half)
        part = jnp.dot(turned[0], own_ref[:, columns], preferred_element_type=F32)
        part += jnp.dot(turned[1], pair_ref[:, columns], preferred_element_type=F32)
        weighted = (part[:tokens] + part[tokens : 2 * tokens]).reshape(sections, rows, half).astype(BF16)
        targeted = part[2 * tokens :].reshape(sections, rows, half).astype(BF16)
        for j in range(pieces):
            lanes = slice(j * LANES, (j + 1) * LANES)
            out_ref[:, t, j] = weighted[:, :, lanes]
            out_ref[:, t, pieces + j] = targeted[:, :, lanes]

    spare = tiles_of(3 * tokens) * LANES - 3 * tokens
    row = [top, total, picked] + ([jnp.zeros((1, spare), F32)] if spare else [])
    row = jnp.concatenate(row, axis=1)
    digits = []
    for _ in range(3):
        digits.append(row.astype(BF16).astype(F32))
        row = row - digits[-1]
    digits.append(jnp.zeros((rows - 3, row.shape[1]), F32))
    digits = jnp.concatenate(digits, axis=0).astype(BF16)
    for j in range(tiles_of(3 * tokens)):
        tile = digits[:, j * LANES : (j + 1) * LANES]
        for t in range(tensors):
            out_ref[:, t, 2 * pieces + j] = jnp.broadcast_to(tile[None], (sections, rows, LANES))


def totals_kernel(
    parts_ref, logits_ref, targets_ref, mask_ref, dlogits_ref, scales_ref, log_total_ref, picked_ref, table_ref
):
    chips = table_ref.shape[0]
    tokens = log_total_ref.shape[1]
    first = parts_ref.shape[1] - tiles_of(3 * tokens)
    for k in range(chips):
        for j in range(tiles_of(3 * tokens)):
            tile = parts_ref[2 * k, first + j].astype(F32)
            table_ref[k : k + 1, j * LANES : (j + 1) * LANES] = jnp.sum(tile, axis=0, keepdims=True)
    table = table_ref[...]
    tops = table[:, :tokens]
    totals = table[:, tokens : 2 * tokens]
    picked = jnp.sum(table[:, 2 * tokens : 3 * tokens], axis=0, keepdims=True)
    row_top = jnp.maximum(jnp.max(tops, axis=0, keepdims=True), picked)
    row_total = jnp.sum(totals * jnp.exp(tops - row_top), axis=0, keepdims=True) + jnp.exp(picked - row_top)
    log_total = row_top + jnp.log(row_total)
    kept = mask_ref[...].astype(F32)
    factor = 1.0 + 2.0 * z_weight * log_total
    hit = target_hits(logits_ref.shape, targets_ref[...], False).astype(F32)
    dlogits_ref[...] = (kept * (factor * jnp.exp(logits_ref[...] - log_total) - hit)).astype(BF16)
    log_total_ref[...] = log_total
    picked_ref[...] = picked

    scales = (kept * (factor * jnp.exp(tops - log_total))).astype(BF16).astype(F32)
    scale = (kept * (factor * jnp.exp(picked - log_total) - 1.0)).astype(BF16).astype(F32)
    spare = scales_ref.shape[1] - chips - 1
    scales_ref[...] = jnp.concatenate([scales, scale, jnp.zeros((spare, tokens), F32)], axis=0).T


def finish_kernel(
    dlogits_ref,
    mine_ref,
    other_ref,
    parts_ref,
    scales_ref,
    log_total_ref,
    picked_ref,
    mask_ref,
    weight_grad_ref,
    hidden_grad_ref,
    ce_ref,
    z_ref,
    blocks_ref,
    shares_ref,
    losses_ref,
    block_sems,
    sems,
):
    sections, tensors, rows, half = mine_ref.shape
    tokens = sections * rows
    chips = sections * tensors // 2
    pieces = half // LANES
    core = this_core()
    copies = []

    def send(source, target, sem):
        copies.append(pltpu.make_async_copy(source, target, sem))
        copies[-1].start()

    log_total = log_total_ref[...]
    kept = mask_ref[...].astype(F32)
    losses_ref[0] = jnp.sum(kept * (log_total - picked_ref[...]), axis=1, keepdims=True) / tokens
    losses_ref[1] = jnp.sum(kept * log_total * log_total, axis=1, keepdims=True) / tokens
    send(losses_ref.at[0], ce_ref, sems.at[0])
    send(losses_ref.at[1], z_ref, sems.at[1])

    here = scales_ref[pl.ds(pl.multiple_of(lax.axis_index("section") * rows, rows), rows), :]

    def share(part, j):
        weighted = jnp.zeros((rows, LANES), F32)
        targeted = jnp.zeros((rows, LANES), F32)
        for k in range(chips):
            weighted += here[:, k : k + 1] * parts_ref[2 * k + part, j].astype(F32)
            targeted += parts_ref[2 * k + part, pieces + j].astype(F32)
        start = part * half + j * LANES
        shares_ref[:, start : start + LANES] = weighted + here[:, chips : chips + 1] * targeted

    dlogits = dlogits_ref[...]
    tasks = [(part, j) for part in range(2) for j in range(pieces)]
    for t in range(tensors):
        for ref, place in ((mine_ref, core), (other_ref, 1 - core)):
            x = ref[:, t].reshape(tokens, half)
            blocks_ref[:, half_columns(t, place, half)] = jnp.dot(
                dlogits, x, preferred_element_type=F32
            ).astype(BF16)
        columns = slice(2 * t * half, 2 * (t + 1) * half)
        send(blocks_ref.at[:, columns], weight_grad_ref.at[:, columns], block_sems.at[t])
        for _ in range(min(len(tasks), -(-2 * pieces // max(tensors - 2, 1)))):
            share(*tasks.pop(0))
            if not tasks:
                send(shares_ref, hidden_grad_ref, sems.at[2])
    for copy in copies:
        copy.wait()


def body(hidden, out_weight, targets, token_mask):
    sections, tensors = lax.axis_size("section"), lax.axis_size("tensor")
    devices = sections * tensors
    vocab_dev, width = out_weight.shape
    rows, block = hidden.shape
    half = block // 2
    tokens = sections * rows
    swap = [(i, i ^ 1) for i in range(tensors)]
    target_row = targets.reshape(1, tokens)
    mask_row = token_mask.reshape(1, tokens)
    flops = 2 * tokens * vocab_dev * width
    tiles = 2 * (half // LANES) + tiles_of(3 * tokens)

    pair_weight = lax.ppermute(out_weight, "tensor", swap)
    sent = pl.pallas_call(
        spread_kernel,
        out_shape=jax.ShapeDtypeStruct((devices, rows, half), BF16),
        in_specs=[VMEM],
        out_specs=VMEM,
        compiler_params=SMALL,
        name="spread_rows",
    )(hidden)
    mine = lax.all_to_all(sent, BOTH, 0, 0)
    mine = mine.reshape(sections, tensors, rows, half)

    half_logits = pl.pallas_call(
        logits_kernel,
        out_shape=jax.ShapeDtypeStruct((vocab_dev, tokens), F32),
        in_specs=[VMEM] * 2,
        out_specs=VMEM,
        compiler_params=SMALL,
        cost_estimate=pl.CostEstimate(flops=flops // 2, bytes_accessed=vocab_dev * width, transcendentals=0),
        name="half_logits",
    )
    pair_mine = half_logits(mine, pair_weight)
    own_other = lax.ppermute(pair_mine, "tensor", swap)
    own_mine = half_logits(mine, out_weight)
    pair_other = lax.ppermute(own_mine, "tensor", swap)
    other = lax.ppermute(mine, "tensor", swap)

    logits, parts = pl.pallas_call(
        parts_kernel,
        out_shape=(
            jax.ShapeDtypeStruct((vocab_dev, tokens), F32),
            jax.ShapeDtypeStruct((sections, tensors, tiles, rows, LANES), BF16),
        ),
        in_specs=[VMEM] * 7,
        out_specs=(VMEM, VMEM),
        compiler_params=SMALL,
        cost_estimate=pl.CostEstimate(
            flops=3 * flops, bytes_accessed=2 * vocab_dev * width, transcendentals=2 * vocab_dev * tokens
        ),
        name="grad_parts",
    )(own_mine, own_other, pair_mine, pair_other, target_row, out_weight, pair_weight)
    parts = lax.all_to_all(parts.reshape(devices, tiles, rows, LANES), BOTH, 0, 0)

    chips = devices // 2
    row = jax.ShapeDtypeStruct((1, tokens), F32)
    dlogits, scales, log_total, picked = pl.pallas_call(
        totals_kernel,
        out_shape=(
            jax.ShapeDtypeStruct((vocab_dev, tokens), BF16),
            jax.ShapeDtypeStruct((tokens, tiles_of(chips + 1) * LANES), F32),
            row,
            row,
        ),
        in_specs=[VMEM] * 4,
        out_specs=(VMEM,) * 4,
        scratch_shapes=[pltpu.VMEM((chips, tiles_of(3 * tokens) * LANES), F32)],
        compiler_params=SMALL,
        cost_estimate=pl.CostEstimate(
            flops=8 * vocab_dev * tokens, bytes_accessed=16 * vocab_dev * tokens, transcendentals=vocab_dev * tokens
        ),
        name="totals",
    )(parts, logits, target_row, mask_row)

    scalar = jax.ShapeDtypeStruct((1, 1), F32)
    grad_weight, grad_hidden, ce_loss, z_loss = pl.pallas_call(
        finish_kernel,
        out_shape=(
            jax.ShapeDtypeStruct((vocab_dev, width), BF16),
            jax.ShapeDtypeStruct((rows, block), F32),
            scalar,
            scalar,
        ),
        in_specs=[VMEM] * 8,
        out_specs=(HBM,) * 4,
        scratch_shapes=[
            pltpu.VMEM((vocab_dev, width), BF16),
            pltpu.VMEM((rows, block), F32),
            pltpu.VMEM((2, 1, 1), F32),
            DMA((tensors,)),
            DMA((3,)),
        ],
        compiler_params=SMALL,
        cost_estimate=pl.CostEstimate(
            flops=flops, bytes_accessed=2 * vocab_dev * width + 2 * tokens * width, transcendentals=0
        ),
        name="finish",
    )(dlogits, mine, other, parts, scales, log_total, picked, mask_row)
    return (ce_loss.reshape(()), z_loss.reshape(()), grad_hidden, grad_weight)


def solution(mesh):
    placed = (P("section", "tensor"), P(("section", "tensor"), None), P(), P())
    return jax.shard_map(
        body,
        mesh=mesh,
        in_specs=placed,
        out_specs=(P(), P(), P("section", "tensor"), P(("section", "tensor"), None)),
        check_vma=False,
    )
```

```python
import jax
import jax.numpy as jnp
from jax import lax
from jax.experimental import pallas as pl
from jax.experimental.pallas import tpu as pltpu
from jax.sharding import PartitionSpec as P


z_weight = 0.0001
BOTH = ("section", "tensor")
LANES = 128
SUB = 4
VMEM = pl.BlockSpec(memory_space=pltpu.VMEM)
HBM = pl.BlockSpec(memory_space=pltpu.HBM)
DMA = pltpu.SemaphoreType.DMA
SMALL = pltpu.CompilerParams(vmem_limit_bytes=16 << 20)
F32, BF16 = jnp.float32, jnp.bfloat16


def tiles_of(count):
    return -(-count // LANES)


def this_core():
    return lax.rem(lax.axis_index("tensor"), 2)


def half_columns(block, core, half):
    return pl.ds(pl.multiple_of((2 * block + core) * half, half), half)


def target_hits(shape, targets, other):
    index = lax.axis_index("section") * lax.axis_size("tensor") + lax.axis_index("tensor")
    if other:
        index = index + 1 - 2 * this_core()
    return lax.broadcasted_iota(jnp.int32, shape, 0) + index * shape[0] == targets


def spread_kernel(hidden_ref, out_ref):
    half = out_ref.shape[2]
    for device in range(out_ref.shape[0]):
        part = device % 2
        out_ref[device] = hidden_ref[:, part * half : (part + 1) * half]


def logits_kernel(rows_ref, weight_ref, out_ref):
    sections, tensors, rows, half = rows_ref.shape
    core = this_core()
    total = jnp.zeros(out_ref.shape, F32)
    for t in range(tensors):
        x = rows_ref[:, t].reshape(sections * rows, half)
        total += lax.dot_general(
            weight_ref[:, half_columns(t, core, half)], x, (((1,), (1,)), ((), ())), preferred_element_type=F32
        )
    out_ref[...] = total


def parts_kernel(
    own_mine_ref, own_other_ref, pair_mine_ref, pair_other_ref, targets_ref, own_ref, pair_ref, logits_ref, out_ref
):
    vocab_dev, tokens = own_mine_ref.shape
    sections, tensors = out_ref.shape[:2]
    rows = tokens // sections
    half = own_ref.shape[1] // tensors // 2
    pieces = half // LANES
    first = 2 * pieces * (rows // SUB)
    core = this_core()
    targets = targets_ref[...]
    logits = (own_mine_ref[...] + own_other_ref[...], pair_mine_ref[...] + pair_other_ref[...])
    logits_ref[...] = logits[0]
    hits = [target_hits((vocab_dev, tokens), targets, other) for other in (False, True)]
    rest = [jnp.where(hit, -jnp.inf, x) for hit, x in zip(hits, logits)]
    top = jnp.maximum(*[jnp.max(x, axis=0, keepdims=True) for x in rest])
    shares = [jnp.exp(x - top) for x in rest]
    total = sum(jnp.sum(x, axis=0, keepdims=True) for x in shares)
    picked = sum(jnp.sum(jnp.where(hit, x, 0.0), axis=0, keepdims=True) for hit, x in zip(hits, logits))

    turned = []
    for share, hit in zip(shares, hits):
        share = share.T
        coarse = share.astype(BF16)
        fine = (share - coarse.astype(F32)).astype(BF16)
        turned.append(jnp.concatenate([coarse, fine, hit.astype(F32).T.astype(BF16)], axis=0))
    for t in range(tensors):
        columns = half_columns(t, core, half)
        part = jnp.dot(turned[0], own_ref[:, columns], preferred_element_type=F32)
        part += jnp.dot(turned[1], pair_ref[:, columns], preferred_element_type=F32)
        weighted = (part[:tokens] + part[tokens : 2 * tokens]).reshape(sections, rows, half).astype(BF16)
        targeted = part[2 * tokens :].reshape(sections, rows, half).astype(BF16)
        for j in range(pieces):
            lanes = slice(j * LANES, (j + 1) * LANES)
            for i in range(rows // SUB):
                some = slice(i * SUB, (i + 1) * SUB)
                tile = j * (rows // SUB) + i
                out_ref[:, t, tile] = weighted[:, some, lanes]
                out_ref[:, t, first // 2 + tile] = targeted[:, some, lanes]

    spare = tiles_of(3 * tokens) * LANES - 3 * tokens
    row = [top, total, picked] + ([jnp.zeros((1, spare), F32)] if spare else [])
    row = jnp.concatenate(row, axis=1)
    digits = []
    for _ in range(3):
        digits.append(row.astype(BF16).astype(F32))
        row = row - digits[-1]
    digits.append(jnp.zeros((SUB - 3, row.shape[1]), F32))
    digits = jnp.concatenate(digits, axis=0).astype(BF16)
    for j in range(tiles_of(3 * tokens)):
        tile = digits[:, j * LANES : (j + 1) * LANES]
        for t in range(tensors):
            out_ref[:, t, first + j] = jnp.broadcast_to(tile[None], (sections, SUB, LANES))


def totals_kernel(
    parts_ref, logits_ref, targets_ref, mask_ref, dlogits_ref, scales_ref, log_total_ref, picked_ref, table_ref
):
    chips = table_ref.shape[0]
    tokens = log_total_ref.shape[1]
    first = parts_ref.shape[1] - tiles_of(3 * tokens)
    for k in range(chips):
        for j in range(tiles_of(3 * tokens)):
            tile = parts_ref[2 * k, first + j].astype(F32)
            table_ref[k : k + 1, j * LANES : (j + 1) * LANES] = jnp.sum(tile, axis=0, keepdims=True)
    table = table_ref[...]
    tops = table[:, :tokens]
    totals = table[:, tokens : 2 * tokens]
    picked = jnp.sum(table[:, 2 * tokens : 3 * tokens], axis=0, keepdims=True)
    row_top = jnp.maximum(jnp.max(tops, axis=0, keepdims=True), picked)
    row_total = jnp.sum(totals * jnp.exp(tops - row_top), axis=0, keepdims=True) + jnp.exp(picked - row_top)
    log_total = row_top + jnp.log(row_total)
    kept = mask_ref[...].astype(F32)
    factor = 1.0 + 2.0 * z_weight * log_total
    hit = target_hits(logits_ref.shape, targets_ref[...], False).astype(F32)
    dlogits_ref[...] = (kept * (factor * jnp.exp(logits_ref[...] - log_total) - hit)).astype(BF16)
    log_total_ref[...] = log_total
    picked_ref[...] = picked

    scales = (kept * (factor * jnp.exp(tops - log_total))).astype(BF16).astype(F32)
    scale = (kept * (factor * jnp.exp(picked - log_total) - 1.0)).astype(BF16).astype(F32)
    spare = scales_ref.shape[1] - chips - 1
    scales_ref[...] = jnp.concatenate([scales, scale, jnp.zeros((spare, tokens), F32)], axis=0).T


def finish_kernel(
    dlogits_ref,
    mine_ref,
    other_ref,
    parts_ref,
    scales_ref,
    log_total_ref,
    picked_ref,
    mask_ref,
    weight_grad_ref,
    hidden_grad_ref,
    ce_ref,
    z_ref,
    blocks_ref,
    shares_ref,
    losses_ref,
    block_sems,
    sems,
):
    sections, tensors, rows, half = mine_ref.shape
    tokens = sections * rows
    chips = sections * tensors // 2
    pieces = half // LANES
    core = this_core()
    copies = []

    def send(source, target, sem):
        copies.append(pltpu.make_async_copy(source, target, sem))
        copies[-1].start()

    log_total = log_total_ref[...]
    kept = mask_ref[...].astype(F32)
    losses_ref[0] = jnp.sum(kept * (log_total - picked_ref[...]), axis=1, keepdims=True) / tokens
    losses_ref[1] = jnp.sum(kept * log_total * log_total, axis=1, keepdims=True) / tokens
    send(losses_ref.at[0], ce_ref, sems.at[0])
    send(losses_ref.at[1], z_ref, sems.at[1])

    here = scales_ref[pl.ds(pl.multiple_of(lax.axis_index("section") * rows, rows), rows), :]

    def share(part, j):
        for i in range(rows // SUB):
            some = slice(i * SUB, (i + 1) * SUB)
            tile = j * (rows // SUB) + i
            weighted = jnp.zeros((SUB, LANES), F32)
            targeted = jnp.zeros((SUB, LANES), F32)
            for k in range(chips):
                weighted += here[some, k : k + 1] * parts_ref[2 * k + part, tile].astype(F32)
                targeted += parts_ref[2 * k + part, pieces * (rows // SUB) + tile].astype(F32)
            start = part * half + j * LANES
            shares_ref[some, start : start + LANES] = weighted + here[some, chips : chips + 1] * targeted

    dlogits = dlogits_ref[...]
    tasks = [(part, j) for part in range(2) for j in range(pieces)]
    for t in range(tensors):
        for ref, place in ((mine_ref, core), (other_ref, 1 - core)):
            x = ref[:, t].reshape(tokens, half)
            blocks_ref[:, half_columns(t, place, half)] = jnp.dot(
                dlogits, x, preferred_element_type=F32
            ).astype(BF16)
        columns = slice(2 * t * half, 2 * (t + 1) * half)
        send(blocks_ref.at[:, columns], weight_grad_ref.at[:, columns], block_sems.at[t])
        for _ in range(min(len(tasks), -(-2 * pieces // max(tensors - 2, 1)))):
            share(*tasks.pop(0))
            if not tasks:
                send(shares_ref, hidden_grad_ref, sems.at[2])
    for copy in copies:
        copy.wait()


def body(hidden, out_weight, targets, token_mask):
    sections, tensors = lax.axis_size("section"), lax.axis_size("tensor")
    devices = sections * tensors
    vocab_dev, width = out_weight.shape
    rows, block = hidden.shape
    half = block // 2
    tokens = sections * rows
    swap = [(i, i ^ 1) for i in range(tensors)]
    target_row = targets.reshape(1, tokens)
    mask_row = token_mask.reshape(1, tokens)
    flops = 2 * tokens * vocab_dev * width
    tiles = 2 * (half // LANES) * (rows // SUB) + tiles_of(3 * tokens)

    pair_weight = lax.ppermute(out_weight, "tensor", swap)
    sent = pl.pallas_call(
        spread_kernel,
        out_shape=jax.ShapeDtypeStruct((devices, rows, half), BF16),
        in_specs=[VMEM],
        out_specs=VMEM,
        compiler_params=SMALL,
        name="spread_rows",
    )(hidden)
    mine = lax.all_to_all(sent, BOTH, 0, 0)
    mine = mine.reshape(sections, tensors, rows, half)

    half_logits = pl.pallas_call(
        logits_kernel,
        out_shape=jax.ShapeDtypeStruct((vocab_dev, tokens), F32),
        in_specs=[VMEM] * 2,
        out_specs=VMEM,
        compiler_params=SMALL,
        cost_estimate=pl.CostEstimate(flops=flops // 2, bytes_accessed=vocab_dev * width, transcendentals=0),
        name="half_logits",
    )
    pair_mine = half_logits(mine, pair_weight)
    own_other = lax.ppermute(pair_mine, "tensor", swap)
    own_mine = half_logits(mine, out_weight)
    pair_other = lax.ppermute(own_mine, "tensor", swap)
    other = lax.ppermute(mine, "tensor", swap)

    logits, parts = pl.pallas_call(
        parts_kernel,
        out_shape=(
            jax.ShapeDtypeStruct((vocab_dev, tokens), F32),
            jax.ShapeDtypeStruct((sections, tensors, tiles, SUB, LANES), BF16),
        ),
        in_specs=[VMEM] * 7,
        out_specs=(VMEM, VMEM),
        compiler_params=SMALL,
        cost_estimate=pl.CostEstimate(
            flops=3 * flops, bytes_accessed=2 * vocab_dev * width, transcendentals=2 * vocab_dev * tokens
        ),
        name="grad_parts",
    )(own_mine, own_other, pair_mine, pair_other, target_row, out_weight, pair_weight)
    parts = lax.all_to_all(parts.reshape(devices, tiles, SUB, LANES), BOTH, 0, 0)

    chips = devices // 2
    row = jax.ShapeDtypeStruct((1, tokens), F32)
    dlogits, scales, log_total, picked = pl.pallas_call(
        totals_kernel,
        out_shape=(
            jax.ShapeDtypeStruct((vocab_dev, tokens), BF16),
            jax.ShapeDtypeStruct((tokens, tiles_of(chips + 1) * LANES), F32),
            row,
            row,
        ),
        in_specs=[VMEM] * 4,
        out_specs=(VMEM,) * 4,
        scratch_shapes=[pltpu.VMEM((chips, tiles_of(3 * tokens) * LANES), F32)],
        compiler_params=SMALL,
        cost_estimate=pl.CostEstimate(
            flops=8 * vocab_dev * tokens, bytes_accessed=16 * vocab_dev * tokens, transcendentals=vocab_dev * tokens
        ),
        name="totals",
    )(parts, logits, target_row, mask_row)

    scalar = jax.ShapeDtypeStruct((1, 1), F32)
    grad_weight, grad_hidden, ce_loss, z_loss = pl.pallas_call(
        finish_kernel,
        out_shape=(
            jax.ShapeDtypeStruct((vocab_dev, width), BF16),
            jax.ShapeDtypeStruct((rows, block), F32),
            scalar,
            scalar,
        ),
        in_specs=[VMEM] * 8,
        out_specs=(HBM,) * 4,
        scratch_shapes=[
            pltpu.VMEM((vocab_dev, width), BF16),
            pltpu.VMEM((rows, block), F32),
            pltpu.VMEM((2, 1, 1), F32),
            DMA((tensors,)),
            DMA((3,)),
        ],
        compiler_params=SMALL,
        cost_estimate=pl.CostEstimate(
            flops=flops, bytes_accessed=2 * vocab_dev * width + 2 * tokens * width, transcendentals=0
        ),
        name="finish",
    )(dlogits, mine, other, parts, scales, log_total, picked, mask_row)
    return (ce_loss.reshape(()), z_loss.reshape(()), grad_hidden, grad_weight)


def solution(mesh):
    placed = (P("section", "tensor"), P(("section", "tensor"), None), P(), P())
    return jax.shard_map(
        body,
        mesh=mesh,
        in_specs=placed,
        out_specs=(P(), P(), P("section", "tensor"), P(("section", "tensor"), None)),
        check_vma=False,
    )
```

```python
import jax
import jax.numpy as jnp
from jax import lax
from jax.experimental import pallas as pl
from jax.experimental.pallas import tpu as pltpu
from jax.sharding import PartitionSpec as P


z_weight = 0.0001
BOTH = ("section", "tensor")
LANES = 128
SUB = 4
VMEM = pl.BlockSpec(memory_space=pltpu.VMEM)
HBM = pl.BlockSpec(memory_space=pltpu.HBM)
DMA = pltpu.SemaphoreType.DMA
SMALL = pltpu.CompilerParams(vmem_limit_bytes=16 << 20)
F32, BF16 = jnp.float32, jnp.bfloat16


def tiles_of(count):
    return -(-count // LANES)


def this_core():
    return lax.rem(lax.axis_index("tensor"), 2)


def half_columns(block, core, half):
    return pl.ds(pl.multiple_of((2 * block + core) * half, half), half)


def target_hits(shape, targets, other):
    index = lax.axis_index("section") * lax.axis_size("tensor") + lax.axis_index("tensor")
    if other:
        index = index + 1 - 2 * this_core()
    return lax.broadcasted_iota(jnp.int32, shape, 0) + index * shape[0] == targets


def spread_kernel(hidden_ref, out_ref):
    half = out_ref.shape[2]
    for device in range(out_ref.shape[0]):
        part = device % 2
        out_ref[device] = hidden_ref[:, part * half : (part + 1) * half]


def logits_kernel(rows_ref, weight_ref, out_ref):
    sections, tensors, rows, half = rows_ref.shape
    core = this_core()
    total = jnp.zeros(out_ref.shape, F32)
    for t in range(tensors):
        x = rows_ref[:, t].reshape(sections * rows, half)
        total += lax.dot_general(
            weight_ref[:, half_columns(t, core, half)], x, (((1,), (1,)), ((), ())), preferred_element_type=F32
        )
    out_ref[...] = total


def parts_kernel(
    own_mine_ref, own_other_ref, pair_mine_ref, pair_other_ref, targets_ref, own_ref, pair_ref, _, logits_ref, out_ref
):
    vocab_dev, tokens = own_mine_ref.shape
    sections, tensors = out_ref.shape[:2]
    rows = tokens // sections
    half = own_ref.shape[1] // tensors // 2
    pieces = half // LANES
    first = 2 * pieces * (rows // SUB)
    core = this_core()
    targets = targets_ref[...]
    logits = (own_mine_ref[...] + own_other_ref[...], pair_mine_ref[...] + pair_other_ref[...])
    logits_ref[...] = logits[0]
    hits = [target_hits((vocab_dev, tokens), targets, other) for other in (False, True)]
    rest = [jnp.where(hit, -jnp.inf, x) for hit, x in zip(hits, logits)]
    top = jnp.maximum(*[jnp.max(x, axis=0, keepdims=True) for x in rest])
    shares = [jnp.exp(x - top) for x in rest]
    total = sum(jnp.sum(x, axis=0, keepdims=True) for x in shares)
    picked = sum(jnp.sum(jnp.where(hit, x, 0.0), axis=0, keepdims=True) for hit, x in zip(hits, logits))

    turned = []
    for share, hit in zip(shares, hits):
        share = share.T
        coarse = share.astype(BF16)
        fine = (share - coarse.astype(F32)).astype(BF16)
        turned.append(jnp.concatenate([coarse, fine, hit.astype(F32).T.astype(BF16)], axis=0))
    for t in range(tensors):
        columns = half_columns(t, core, half)
        part = jnp.dot(turned[0], own_ref[:, columns], preferred_element_type=F32)
        part += jnp.dot(turned[1], pair_ref[:, columns], preferred_element_type=F32)
        weighted = (part[:tokens] + part[tokens : 2 * tokens]).reshape(sections, rows, half).astype(BF16)
        targeted = part[2 * tokens :].reshape(sections, rows, half).astype(BF16)
        for j in range(pieces):
            lanes = slice(j * LANES, (j + 1) * LANES)
            for i in range(rows // SUB):
                some = slice(i * SUB, (i + 1) * SUB)
                tile = j * (rows // SUB) + i
                out_ref[:, t, tile] = weighted[:, some, lanes]
                out_ref[:, t, first // 2 + tile] = targeted[:, some, lanes]

    spare = tiles_of(3 * tokens) * LANES - 3 * tokens
    row = [top, total, picked] + ([jnp.zeros((1, spare), F32)] if spare else [])
    row = jnp.concatenate(row, axis=1)
    digits = []
    for _ in range(3):
        digits.append(row.astype(BF16).astype(F32))
        row = row - digits[-1]
    digits.append(jnp.zeros((SUB - 3, row.shape[1]), F32))
    digits = jnp.concatenate(digits, axis=0).astype(BF16)
    for j in range(tiles_of(3 * tokens)):
        tile = digits[:, j * LANES : (j + 1) * LANES]
        for t in range(tensors):
            out_ref[:, t, first + j] = jnp.broadcast_to(tile[None], (sections, SUB, LANES))


def finish_kernel(
    parts_ref,
    logits_ref,
    targets_ref,
    mask_ref,
    mine_ref,
    other_ref,
    weight_grad_ref,
    hidden_grad_ref,
    ce_ref,
    z_ref,
    table_ref,
    scales_ref,
    blocks_ref,
    shares_ref,
    losses_ref,
    block_sems,
    sems,
):
    sections, tensors, rows, half = mine_ref.shape
    tokens = sections * rows
    chips = sections * tensors // 2
    pieces = half // LANES
    core = this_core()
    copies = []

    def send(source, target, sem):
        copies.append(pltpu.make_async_copy(source, target, sem))
        copies[-1].start()

    first = parts_ref.shape[1] - tiles_of(3 * tokens)
    for k in range(chips):
        for j in range(tiles_of(3 * tokens)):
            tile = parts_ref[2 * k, first + j].astype(F32)
            table_ref[k : k + 1, j * LANES : (j + 1) * LANES] = jnp.sum(tile, axis=0, keepdims=True)
    table = table_ref[...]
    tops = table[:, :tokens]
    totals = table[:, tokens : 2 * tokens]
    picked = jnp.sum(table[:, 2 * tokens : 3 * tokens], axis=0, keepdims=True)
    row_top = jnp.maximum(jnp.max(tops, axis=0, keepdims=True), picked)
    row_total = jnp.sum(totals * jnp.exp(tops - row_top), axis=0, keepdims=True) + jnp.exp(picked - row_top)
    log_total = row_top + jnp.log(row_total)
    kept = mask_ref[...].astype(F32)
    factor = 1.0 + 2.0 * z_weight * log_total
    hit = target_hits(logits_ref.shape, targets_ref[...], False).astype(F32)
    dlogits = (kept * (factor * jnp.exp(logits_ref[...] - log_total) - hit)).astype(BF16)

    scales = (kept * (factor * jnp.exp(tops - log_total))).astype(BF16).astype(F32)
    scale = (kept * (factor * jnp.exp(picked - log_total) - 1.0)).astype(BF16).astype(F32)
    spare = scales_ref.shape[1] - chips - 1
    scales_ref[...] = jnp.concatenate([scales, scale, jnp.zeros((spare, tokens), F32)], axis=0).T

    losses_ref[0] = jnp.sum(kept * (log_total - picked), axis=1, keepdims=True) / tokens
    losses_ref[1] = jnp.sum(kept * log_total * log_total, axis=1, keepdims=True) / tokens
    send(losses_ref.at[0], ce_ref, sems.at[0])
    send(losses_ref.at[1], z_ref, sems.at[1])

    here = scales_ref[pl.ds(pl.multiple_of(lax.axis_index("section") * rows, rows), rows), :]

    def share(part, j):
        for i in range(rows // SUB):
            some = slice(i * SUB, (i + 1) * SUB)
            tile = j * (rows // SUB) + i
            weighted = jnp.zeros((SUB, LANES), F32)
            targeted = jnp.zeros((SUB, LANES), F32)
            for k in range(chips):
                weighted += here[some, k : k + 1] * parts_ref[2 * k + part, tile].astype(F32)
                targeted += parts_ref[2 * k + part, pieces * (rows // SUB) + tile].astype(F32)
            start = part * half + j * LANES
            shares_ref[some, start : start + LANES] = weighted + here[some, chips : chips + 1] * targeted

    tasks = [(part, j) for part in range(2) for j in range(pieces)]
    for t in range(tensors):
        for ref, place in ((mine_ref, core), (other_ref, 1 - core)):
            x = ref[:, t].reshape(tokens, half)
            blocks_ref[:, half_columns(t, place, half)] = jnp.dot(
                dlogits, x, preferred_element_type=F32
            ).astype(BF16)
        columns = slice(2 * t * half, 2 * (t + 1) * half)
        send(blocks_ref.at[:, columns], weight_grad_ref.at[:, columns], block_sems.at[t])
        for _ in range(min(len(tasks), -(-2 * pieces // max(tensors - 2, 1)))):
            share(*tasks.pop(0))
            if not tasks:
                send(shares_ref, hidden_grad_ref, sems.at[2])
    for copy in copies:
        copy.wait()


def body(hidden, out_weight, targets, token_mask):
    sections, tensors = lax.axis_size("section"), lax.axis_size("tensor")
    devices = sections * tensors
    vocab_dev, width = out_weight.shape
    rows, block = hidden.shape
    half = block // 2
    tokens = sections * rows
    swap = [(i, i ^ 1) for i in range(tensors)]
    target_row = targets.reshape(1, tokens)
    mask_row = token_mask.reshape(1, tokens)
    flops = 2 * tokens * vocab_dev * width
    tiles = 2 * (half // LANES) * (rows // SUB) + tiles_of(3 * tokens)

    pair_weight = lax.ppermute(out_weight, "tensor", swap)
    sent = pl.pallas_call(
        spread_kernel,
        out_shape=jax.ShapeDtypeStruct((devices, rows, half), BF16),
        in_specs=[VMEM],
        out_specs=VMEM,
        compiler_params=SMALL,
        name="spread_rows",
    )(hidden)
    mine = lax.all_to_all(sent, BOTH, 0, 0)
    mine = mine.reshape(sections, tensors, rows, half)

    half_logits = pl.pallas_call(
        logits_kernel,
        out_shape=jax.ShapeDtypeStruct((vocab_dev, tokens), F32),
        in_specs=[VMEM] * 2,
        out_specs=VMEM,
        compiler_params=SMALL,
        cost_estimate=pl.CostEstimate(flops=flops // 2, bytes_accessed=vocab_dev * width, transcendentals=0),
        name="half_logits",
    )
    pair_mine = half_logits(mine, pair_weight)
    own_other = lax.ppermute(pair_mine, "tensor", swap)
    own_mine = half_logits(mine, out_weight)
    pair_other = lax.ppermute(own_mine, "tensor", swap)
    other = lax.ppermute(mine, "tensor", swap)

    logits, parts = pl.pallas_call(
        parts_kernel,
        out_shape=(
            jax.ShapeDtypeStruct((vocab_dev, tokens), F32),
            jax.ShapeDtypeStruct((sections, tensors, tiles, SUB, LANES), BF16),
        ),
        in_specs=[VMEM] * 7 + [pl.BlockSpec(memory_space=pl.ANY)],
        out_specs=(VMEM, VMEM),
        compiler_params=SMALL,
        cost_estimate=pl.CostEstimate(
            flops=3 * flops, bytes_accessed=2 * vocab_dev * width, transcendentals=2 * vocab_dev * tokens
        ),
        name="grad_parts",
    )(own_mine, own_other, pair_mine, pair_other, target_row, out_weight, pair_weight, other)
    parts = lax.all_to_all(parts.reshape(devices, tiles, SUB, LANES), BOTH, 0, 0)

    chips = devices // 2
    scalar = jax.ShapeDtypeStruct((1, 1), F32)
    grad_weight, grad_hidden, ce_loss, z_loss = pl.pallas_call(
        finish_kernel,
        out_shape=(
            jax.ShapeDtypeStruct((vocab_dev, width), BF16),
            jax.ShapeDtypeStruct((rows, block), F32),
            scalar,
            scalar,
        ),
        in_specs=[VMEM] * 6,
        out_specs=(HBM,) * 4,
        scratch_shapes=[
            pltpu.VMEM((chips, tiles_of(3 * tokens) * LANES), F32),
            pltpu.VMEM((tokens, tiles_of(chips + 1) * LANES), F32),
            pltpu.VMEM((vocab_dev, width), BF16),
            pltpu.VMEM((rows, block), F32),
            pltpu.VMEM((2, 1, 1), F32),
            DMA((tensors,)),
            DMA((3,)),
        ],
        compiler_params=SMALL,
        cost_estimate=pl.CostEstimate(
            flops=flops, bytes_accessed=2 * vocab_dev * width + 2 * tokens * width, transcendentals=0
        ),
        name="finish",
    )(parts, logits, target_row, mask_row, mine, other)
    return (ce_loss.reshape(()), z_loss.reshape(()), grad_hidden, grad_weight)


def solution(mesh):
    placed = (P("section", "tensor"), P(("section", "tensor"), None), P(), P())
    return jax.shard_map(
        body,
        mesh=mesh,
        in_specs=placed,
        out_specs=(P(), P(), P("section", "tensor"), P(("section", "tensor"), None)),
        check_vma=False,
    )
```
